32 devices in a mesh: rows: 8 (over z, y), cols: 4 (over x, core).
Axes of the slice: x: 2, y: 2, z: 4, core: 2. Of those that a mesh axis runs over, the one named last changes fastest.
Arguments:
- coefficients: float32 [4, 1024, 4, 256], P(None, 'rows'), may hold values from -0.03 to 0.09
- support: int32 [4, 1024, 4], P(None, 'rows'), may hold values from 0 to 11, all different within a row
- primal: float32 [12, 256, 256], P('cols'), may hold values from -0.5 to 9, as said below
- dual_inverse: float32 [12, 256, 256], P('cols'), may hold values from -0.5 to 9, as said below
- block_sizes: int32 [12], P('cols'), may hold values from 64 to 256, as said below
- damping: float32 [4, 1024], P(None, 'rows'), may hold values from 0.5 to 2
- right_sides: float32 [4, 32, 1024], P(None, 'cols', 'rows'), may hold values from -6 to 6
Outputs:
- updated: float32 [4, 1024, 4096], P(None, 'rows', 'cols')
- panel_factor: float32 [4, 1024, 128], P(None, 'rows')
- solved: float32 [4, 32, 1024], P(None, 'cols', 'rows')
The draws below stay inside these ranges and needn't reach their ends.
Inputs may be any that keep to these rules, and one draw needn't show every extreme that they name: `primal`: each block is symmetric positive definite. `dual_inverse`: each block is symmetric positive definite. `block_sizes`: some block has order 256.
All inputs are finite; a program needn't handle non-finite values.
Results may differ from the reference program's by a relative error of at most 0.00015.
Values sent between devices are 32-bit elements; how exact they have to be, the bound alone decides.
A program may use at most 192 MiB of HBM per device.

```python
import math
import jax
import jax.numpy as jnp
from jax import lax

BS = 256
K = 4
TILE = 128
NRHS = 32
TPR = 4
SPAN = 1024
NB = 12
N_ROWS = 8


def definite_blocks(key):
    first_key, second_key = jax.random.split(key)
    floor_value, ceiling, spread = (1.0, 4.0, 0.4)
    diagonal = jnp.exp(jax.random.uniform(first_key, (NB, BS), jnp.float32, math.log(floor_value), math.log(ceiling)))
    noise = jax.random.normal(second_key, (NB, BS, BS), jnp.float32) * (spread / math.sqrt(BS))
    symmetric = (noise + jnp.swapaxes(noise, 1, 2)) / math.sqrt(2.0)
    return symmetric + diagonal[:, :, None] * jnp.eye(BS, dtype=jnp.float32)[None, :, :]


def draw_primal(key, part):
    return definite_blocks(jax.random.fold_in(key, 11))


def draw_dual_inverse(key, part):
    return definite_blocks(jax.random.fold_in(key, 23))


def draw_block_sizes(key, part):
    orders = jax.random.randint(jax.random.fold_in(key, 31), (NB,), BS // 4, BS + 1)
    picked = jax.random.randint(jax.random.fold_in(key, 37), (), 0, NB)
    return jnp.where(jnp.arange(NB) == picked, BS, orders).astype(jnp.int32)


def block_levels(rng, extent, pieces, least, high):
    loudness, own = 1.0, jax.random.fold_in(rng, 6)
    for position, blocks in pieces:
        draws = jnp.exp(jax.random.uniform(jax.random.fold_in(own, position), (blocks,), jnp.float32, least / len(pieces), high / len(pieces)))
        loudness = loudness * jnp.repeat(draws, extent[position] // blocks).reshape([-1 if axis == position else 1 for axis in range(len(extent))])
    return loudness


def different_ones(stream_key, rows, number_of, top, lift):
    sequence = jax.random.permutation(jax.random.fold_in(stream_key, 1), number_of)
    pull = sequence
    for power in range(3):
        pull = pull * pull // number_of
    pull = pull * lift // number_of
    chance = jax.random.randint(jax.random.fold_in(stream_key, 2), (rows, number_of), 0, 4096) + pull
    fixed_rows = jax.random.permutation(jax.random.fold_in(stream_key, 3), rows)[jnp.arange(number_of) % rows]
    chance = jnp.where(jnp.arange(rows)[:, None] == fixed_rows[None, :], 1 << 14, chance)
    merit = chance * number_of + jnp.arange(number_of)
    return lax.top_k(merit.astype(jnp.int32), top)[1].astype(jnp.int32)


def gaussian(stream_key, extent, scale, reach, pieces=(), kind=jnp.bfloat16):
    drawn = jax.random.normal(stream_key, extent, jnp.float32) * scale
    if len(pieces) > 0:
        drawn = block_levels(stream_key, extent, pieces, -0.22, 0.18) * drawn
    return jnp.clip(drawn, min=-reach, max=reach).astype(kind)


def setup_inputs(seed: int = 0) -> dict:
    streams_of = jax.random.split(jax.random.key(seed), 8)
    return {
        "coefficients": jnp.clip(-0.03 + 0.120000003 * jax.random.uniform(streams_of[0], (TPR, SPAN, K, BS), jnp.float32) ** block_levels(streams_of[0], (TPR, SPAN, K, BS), ((1, 8),), -0.2, 0.2), -0.03, 0.09),
        "support": different_ones(streams_of[1], TPR * SPAN, NB, K, 5461).reshape((TPR, SPAN, K)),
        "primal": draw_primal(jax.random.fold_in(streams_of[7], 71), 0),
        "dual_inverse": draw_dual_inverse(jax.random.fold_in(streams_of[7], 71), 0),
        "block_sizes": draw_block_sizes(jax.random.fold_in(streams_of[7], 71), 0),
        "damping": jnp.clip(jnp.exp(math.log(2.0) - 1.3862944 * jax.random.uniform(streams_of[5], (TPR, SPAN), jnp.float32) ** block_levels(streams_of[5], (TPR, SPAN), ((1, 8),), -0.2, 0.2)), 0.5, 2.0),
        "right_sides": gaussian(streams_of[6], (TPR, NRHS, SPAN), 1.0, 6.0, ((1, 4), (2, 8)), jnp.float32),
    }


highest = lax.Precision.HIGHEST

def reference(coefficients, support, primal, dual_inverse, block_sizes, damping, right_sides):
    count_all = TPR * TILE * N_ROWS
    flat_coef = coefficients.reshape(count_all, K, BS)
    flat_support = support.reshape(count_all, K)
    positions = jnp.arange(BS, dtype=jnp.int32)
    schur_full = jnp.zeros((count_all, count_all), jnp.float32)
    for block_id in range(NB):
        chosen = (flat_support == block_id).astype(jnp.float32)
        dense_rows = jnp.einsum('mk,mkd->md', chosen, flat_coef, precision=highest)
        active = (positions < block_sizes[block_id]).astype(jnp.float32)
        weights = primal[block_id] * dual_inverse[block_id] * active[:, None] * active[None, :]
        weighted = jnp.dot(dense_rows.astype(jnp.float32), weights.astype(jnp.float32), precision=highest, preferred_element_type=jnp.float32)
        schur_full = schur_full + jnp.dot(weighted.astype(jnp.float32), dense_rows.T.astype(jnp.float32), precision=highest, preferred_element_type=jnp.float32)
    schur_full = schur_full + jnp.diag(damping.reshape(count_all))
    corner = schur_full[:TILE, :TILE]
    factor = jnp.linalg.cholesky(corner)
    identity = jnp.eye(TILE, dtype=jnp.float32)
    inverse = jax.scipy.linalg.solve_triangular(factor, identity, lower=True)
    panel_rows = jnp.dot(schur_full[:, :TILE].astype(jnp.float32), inverse.T.astype(jnp.float32), precision=highest, preferred_element_type=jnp.float32)
    outer_term = jnp.dot(panel_rows.astype(jnp.float32), panel_rows.T.astype(jnp.float32), precision=highest, preferred_element_type=jnp.float32)
    later = jnp.arange(count_all) >= TILE
    updated = schur_full - jnp.where(later[:, None] & later[None, :], outer_term, 0.0)
    all_sides = jnp.transpose(right_sides, (1, 0, 2)).reshape(NRHS, count_all)
    leading = jnp.dot(all_sides[:, :TILE].astype(jnp.float32), inverse.T.astype(jnp.float32), precision=highest, preferred_element_type=jnp.float32)
    remainder = all_sides - jnp.dot(leading.astype(jnp.float32), panel_rows.T.astype(jnp.float32), precision=highest, preferred_element_type=jnp.float32)
    padded_lead = jnp.pad(leading, ((0, 0), (0, count_all - TILE)))
    solved = jnp.where(later[None, :], remainder, padded_lead)
    solved = jnp.transpose(solved.reshape(NRHS, TPR, N_ROWS * TILE), (1, 0, 2))
    return (updated.reshape(TPR, N_ROWS * TILE, count_all), panel_rows.reshape(TPR, N_ROWS * TILE, TILE), solved)
```

```python
import functools

import jax
import jax.numpy as jnp
from jax import lax
from jax.experimental import pallas as pl
from jax.experimental.pallas import tpu as pltpu
from jax.sharding import PartitionSpec as P

TILE = 128

MESH = pl.DeviceIdType.MESH
highest = lax.Precision.HIGHEST
high = lax.Precision.HIGH


def exchange(rows, cols, tile_ref, names_ref, lead_ref, small_ref, w_ref, tiles_out, names_out, leads_out, small_out, w_out,
             local_sem, fwd_s, fwd_r, bwd_s, bwd_r, name_s, name_r, lead_s, lead_r, share_s, share_r, small_s, small_r,
             wx_s, wx_r, wp_s, wp_r):
    r = lax.axis_index("rows")
    c = lax.axis_index("cols")
    half = rows // 2
    odd = r % 2
    pos = (1 - odd) * (r // 2) + odd * (rows - 1 - r // 2)

    def row_at(p):
        p = (p + rows) % rows
        upper = p // half
        return (1 - upper) * (2 * p) + upper * (2 * (rows - 1 - p) + 1)

    right = row_at(pos + 1)
    left = row_at(pos - 1)
    partner = c + 1 - 2 * (c % 2)

    def send(src, dst, s, v, row=None, col=None):
        return pltpu.make_async_remote_copy(
            src_ref=src, dst_ref=dst, send_sem=s, recv_sem=v,
            device_id=(r if row is None else row, c if col is None else col), device_id_type=MESH)

    barrier = pltpu.get_barrier_semaphore()
    for d in range(1, rows):
        pl.semaphore_signal(barrier, inc=1, device_id=((r + d) % rows, c), device_id_type=MESH)
    for d in range(1, cols):
        pl.semaphore_signal(barrier, inc=1, device_id=(r, (c + d) % cols), device_id_type=MESH)
    pl.semaphore_wait(barrier, rows + cols - 2)

    slots = tile_ref.shape[0]
    cut = slots // 2
    part = (pl.ds(0, cut), pl.ds(cut, slots - cut))

    own = [pltpu.make_async_copy(tile_ref, tiles_out.at[r], local_sem.at[0]),
           pltpu.make_async_copy(names_ref, names_out.at[r], local_sem.at[1]),
           pltpu.make_async_copy(w_ref, w_out.at[c], local_sem.at[2])]
    for copy in own:
        copy.start()

    waits = []
    for k in range(1, cols // 2):
        copy = send(w_ref, w_out.at[c], wx_s.at[k], wx_r.at[k], col=(c + 2 * k) % cols)
        copy.start()
        waits.append(copy)
    copy = send(w_ref, w_out.at[c], wp_s.at[0], wp_r.at[0], col=partner)
    copy.start()
    waits.append(copy)

    for d in range(1, rows):
        copy = send(names_ref, names_out.at[r], name_s.at[d], name_r.at[d], row=(r + d) % rows)
        copy.start()
        waits.append(copy)

    lead_row = [send(lead_ref, leads_out.at[c], lead_s.at[0], lead_r.at[0], row=right),
                send(lead_ref, leads_out.at[c], lead_s.at[1], lead_r.at[0], row=left)]

    @pl.when(r == 0)
    def _():
        for copy in lead_row:
            copy.start()
        for d in range(1, rows):
            send(small_ref, small_out, small_s.at[d], small_r.at[0], row=d).start()
        pltpu.make_async_copy(lead_ref, leads_out.at[c], local_sem.at[3]).start()
        pltpu.make_async_copy(small_ref, small_out, local_sem.at[4]).start()

    def first(h):
        send(tile_ref.at[part[h]], tiles_out.at[r, part[h]], fwd_s.at[0, h], fwd_r.at[0, h], row=right).start()
        send(tile_ref.at[part[h]], tiles_out.at[r, part[h]], bwd_s.at[0, h], bwd_r.at[0, h], row=left).start()

    first(0)
    near = jnp.minimum(pos, rows - pos)

    @pl.when(near >= 2)
    def _():
        first(1)

    relay_right = send(leads_out.at[c], leads_out.at[c], lead_s.at[0], lead_r.at[0], row=right)
    relay_left = send(leads_out.at[c], leads_out.at[c], lead_s.at[1], lead_r.at[0], row=left)

    @pl.when(r != 0)
    def _():
        relay_right.wait_recv()

    @pl.when((pos >= 1) & (pos < half))
    def _():
        relay_right.start()

    @pl.when(pos >= half + 2)
    def _():
        relay_left.start()

    @pl.when(r == 0)
    def _():
        pltpu.make_async_copy(lead_ref, leads_out.at[c], local_sem.at[3]).wait()
        pltpu.make_async_copy(small_ref, small_out, local_sem.at[4]).wait()

    for d in range(1, cols):
        copy = send(leads_out.at[c], leads_out.at[c], share_s.at[d], share_r.at[d], col=(c + d) % cols)
        copy.start()
        waits.append(copy)

    @pl.when(near < 2)
    def _():
        first(1)

    for k in range(1, cols // 2):
        send(w_ref, w_out.at[c], wx_s.at[k], wx_r.at[k], col=(c + 2 * k) % cols).wait_recv()
        source = (c + cols - 2 * k) % cols
        copy = send(w_out.at[source], w_out.at[source], wp_s.at[k], wp_r.at[k], col=partner)
        copy.start()
        waits.append(copy)

    last = half - 1
    for s in range(1, half):
        for h in range(2):
            ahead = row_at(pos - s)
            behind = row_at(pos + s)
            send(tile_ref.at[part[h]], tiles_out.at[r, part[h]], fwd_s.at[s - 1, h], fwd_r.at[s - 1, h], row=right).wait_recv()
            if s < last or h == 0:
                send(tiles_out.at[ahead, part[h]], tiles_out.at[ahead, part[h]], fwd_s.at[s, h], fwd_r.at[s, h], row=right).start()
            send(tile_ref.at[part[h]], tiles_out.at[r, part[h]], bwd_s.at[s - 1, h], bwd_r.at[s - 1, h], row=left).wait_recv()
            if s < last or h == 1:
                send(tiles_out.at[behind, part[h]], tiles_out.at[behind, part[h]], bwd_s.at[s, h], bwd_r.at[s, h], row=left).start()
    send(tile_ref.at[part[0]], tiles_out.at[r, part[0]], fwd_s.at[last, 0], fwd_r.at[last, 0], row=right).wait_recv()
    send(tile_ref.at[part[1]], tiles_out.at[r, part[1]], bwd_s.at[last, 1], bwd_r.at[last, 1], row=left).wait_recv()

    for s in range(half):
        for h in range(2):
            if s < last or h == 0:
                send(tile_ref.at[part[h]], tiles_out.at[r, part[h]], fwd_s.at[s, h], fwd_r.at[s, h], row=right).wait_send()
            if s < last or h == 1:
                send(tile_ref.at[part[h]], tiles_out.at[r, part[h]], bwd_s.at[s, h], bwd_r.at[s, h], row=left).wait_send()

    for copy in waits:
        copy.wait_send()
    for d in range(1, rows):
        send(names_ref, names_out.at[r], name_s.at[d], name_r.at[d], row=(r + d) % rows).wait_recv()
    for d in range(1, cols):
        send(leads_out.at[c], leads_out.at[c], share_s.at[d], share_r.at[d], col=(c + d) % cols).wait_recv()
    for k in range(cols // 2):
        send(w_ref, w_out.at[c], wp_s.at[k], wp_r.at[k], col=partner).wait_recv()

    @pl.when(r == 0)
    def _():
        for copy in lead_row:
            copy.wait_send()
        for d in range(1, rows):
            send(small_ref, small_out, small_s.at[d], small_r.at[0], row=d).wait_send()

    @pl.when(r != 0)
    def _():
        send(small_ref, small_out, small_s.at[0], small_r.at[0], row=0).wait_recv()

    @pl.when((pos >= 1) & (pos < half))
    def _():
        relay_right.wait_send()

    @pl.when(pos >= half + 2)
    def _():
        relay_left.wait_send()

    for copy in own:
        copy.wait()


def gather_all(rows, cols, tile, names, lead, small, weights):
    half = rows // 2
    dma = pltpu.SemaphoreType.DMA
    vmem = pl.BlockSpec(memory_space=pltpu.VMEM)
    shapes = [(rows,) + tile.shape, (rows,) + names.shape, (cols,) + lead.shape, small.shape, (cols,) + weights.shape]
    kinds = [tile.dtype, names.dtype, lead.dtype, small.dtype, weights.dtype]
    return pl.pallas_call(
        functools.partial(exchange, rows, cols),
        out_shape=[jax.ShapeDtypeStruct(s, k) for s, k in zip(shapes, kinds)],
        in_specs=[vmem] * 5,
        out_specs=[vmem] * 5,
        scratch_shapes=[dma((5,))] + [dma((half, 2))] * 4 + [dma((rows,))] * 2 + [dma((2,)), dma((1,))]
        + [dma((cols,))] * 2 + [dma((rows,)), dma((1,))] + [dma((cols,))] * 4,
        compiler_params=pltpu.CompilerParams(collective_id=0, has_side_effects=True),
    )(tile, names, lead, small, weights)


def densify(values, labels, blocks):
    ids = jnp.arange(blocks, dtype=jnp.int32)
    dense = 0.0
    for j in range(values.shape[0]):
        hit = labels[j][:, None, None] == ids[None, :, None]
        dense = dense + jnp.where(hit, values[j][:, None, :], 0.0)
    return dense


def local(coefficients, support, primal, dual_inverse, block_sizes, damping, right_sides):
    col_index = lax.axis_index("cols")
    row_index = lax.axis_index("rows")
    rows = lax.axis_size("rows")
    cols = lax.axis_size("cols")
    layers, _, slots, order = coefficients.shape
    span = TILE * rows
    count_all = layers * span
    col_width = count_all // cols
    blocks = primal.shape[0] * cols
    sides = right_sides.shape[1]
    positions = jnp.arange(order, dtype=jnp.int32)
    active = (positions[None, :] < block_sizes[:, None]).astype(jnp.float32)
    weights = primal * dual_inverse * active[:, :, None] * active[:, None, :]

    layer = (col_index * col_width) // span
    tile = jnp.transpose(lax.dynamic_index_in_dim(coefficients, layer, 0, keepdims=False), (1, 0, 2))
    own_names = jnp.transpose(support, (0, 2, 1))
    names = jnp.pad(lax.dynamic_index_in_dim(own_names, layer, 0, keepdims=False), ((0, 8 - slots), (0, 0)))
    chunk = TILE // cols
    lead = jnp.transpose(lax.dynamic_slice_in_dim(coefficients[0], col_index * chunk, chunk, 0), (1, 0, 2))
    small = jnp.concatenate([
        jnp.pad(own_names[0].astype(jnp.float32), ((0, 7 - slots), (0, 0))),
        damping[0][None, :],
        jnp.pad(right_sides[0], ((0, -sides % 8), (0, 0)))], axis=0)
    tiles, every_name, leads, small, every_weight = gather_all(rows, cols, tile, names, lead, small, weights)

    every_weight = every_weight.reshape(blocks, order, order)
    lead_coef = jnp.transpose(leads, (1, 0, 2, 3)).reshape(slots, TILE, order)
    lead_names = small[:slots].astype(jnp.int32)
    lead_damping = small[7]
    top_sides = small[8:8 + sides]

    column_coef = jnp.transpose(tiles, (1, 0, 2, 3)).reshape(slots, span, order)
    column_names = jnp.transpose(every_name[:, :slots], (1, 0, 2)).reshape(slots, span)
    if span != col_width:
        start = (col_index * col_width) % span
        column_coef = lax.dynamic_slice_in_dim(column_coef, start, col_width, 1)
        column_names = lax.dynamic_slice_in_dim(column_names, start, col_width, 1)
    column_dense = densify(column_coef, column_names, blocks)
    row_coef = jnp.concatenate([jnp.transpose(coefficients, (2, 0, 1, 3)).reshape(slots, layers * TILE, order), lead_coef], axis=1)
    row_names = jnp.concatenate([jnp.transpose(own_names, (1, 0, 2)).reshape(slots, layers * TILE), lead_names], axis=1)
    row_dense = densify(row_coef, row_names, blocks)
    weighted = jnp.einsum("aqd,qde->aqe", row_dense, every_weight, precision=high)
    schur_rows = jnp.einsum("aqe,nqe->an", weighted, column_dense, precision=high)
    lead_dense = row_dense[layers * TILE:]
    own_lead = jnp.einsum("aqe,nqe->an", weighted, lead_dense, precision=high)

    row_global = ((jnp.arange(layers)[:, None] * rows + row_index) * TILE + jnp.arange(TILE)[None, :]).reshape(-1)
    col_global = col_index * col_width + jnp.arange(col_width)
    flat_damping = damping.reshape(-1)
    eye = jnp.eye(TILE, dtype=jnp.float32)
    corner = own_lead[layers * TILE:] + eye * lead_damping[:, None]
    schur = schur_rows[:layers * TILE] + jnp.where(row_global[:, None] == col_global[None, :], flat_damping[:, None], 0.0)
    lead_ids = jnp.arange(TILE)
    panel_raw = own_lead[:layers * TILE] + jnp.where(row_global[:, None] == lead_ids[None, :], flat_damping[:, None], 0.0)
    column_raw = schur_rows[layers * TILE:] + jnp.where(lead_ids[:, None] == col_global[None, :], lead_damping[:, None], 0.0)
    factor = jnp.linalg.cholesky(corner)
    inverse = jax.scipy.linalg.solve_triangular(factor, eye, lower=True)
    panel_factor = jnp.einsum("ak,jk->aj", panel_raw, inverse, precision=high)
    column_panel = jnp.einsum("jk,kn->jn", inverse, column_raw, precision=high)
    outer_term = jnp.dot(panel_factor, column_panel, precision=high)
    row_later = row_global >= TILE
    col_later = col_global >= TILE
    updated = schur - jnp.where(row_later[:, None] & col_later[None, :], outer_term, 0.0)
    leading = jnp.einsum("sk,jk->sj", top_sides, inverse, precision=high)
    panel_factor = panel_factor.reshape(layers, TILE, TILE)
    remainder = right_sides - jnp.einsum("sk,tak->tsa", leading, panel_factor, precision=high)
    solved = jnp.where(row_later.reshape(layers, TILE)[:, None, :], remainder, leading[None, :, :])
    return (updated.reshape(layers, TILE, col_width), panel_factor, solved)


def solution(mesh):
    in_specs = (
        P(None, "rows", None, None),
        P(None, "rows", None),
        P("cols", None, None),
        P("cols", None, None),
        P("cols"),
        P(None, "rows"),
        P(None, "cols", "rows"),
    )
    out_specs = (P(None, "rows", "cols"), P(None, "rows", None), P(None, "cols", "rows"))
    return jax.shard_map(local, mesh=mesh, in_specs=in_specs, out_specs=out_specs, check_vma=False)
```

```python
import functools

import jax
import jax.numpy as jnp
from jax import lax
from jax.experimental import pallas as pl
from jax.experimental.pallas import tpu as pltpu
from jax.sharding import PartitionSpec as P

TILE = 128

MESH = pl.DeviceIdType.MESH
highest = lax.Precision.HIGHEST


def split(x):
    top = x.astype(jnp.bfloat16)
    return top, (x - top.astype(jnp.float32)).astype(jnp.bfloat16)


def product(a, b, dims):
    return lax.dot_general(a, b, (dims, ((), ())), preferred_element_type=jnp.float32)


def three(a_top, a_low, b_top, b_low, dims):
    return product(a_top, b_top, dims) + (product(a_top, b_low, dims) + product(a_low, b_top, dims))


def select_block(coef, label, b):
    pieces = []
    for h in range(0, 2):
        acc = None
        for k in range(coef.slots):
            hit = label(k) == b
            value = coef(k, h)
            acc = jnp.where(hit, value, jnp.zeros_like(value) if acc is None else acc)
        pieces.append(acc)
    return jnp.concatenate(pieces, axis=1)


class Rows:
    def __init__(self, read, slots):
        self.read, self.slots = read, slots

    def __call__(self, k, h):
        return self.read(k, pl.ds(h * TILE, TILE))


def exchange(rows, cols, tile_ref, names_ref, lead_ref, small_ref, w_ref, own_ref, own_names_ref,
             schur_out, lead_schur_out, inverse_out, small_out,
             tiles_out, names_out, leads_out, w_out, label_own, label_col, lead_sc, d_top, d_low, c_top, c_low,
             g_top, g_low, acc, work,
             local_sem, fwd_s, fwd_r, bwd_s, bwd_r, name_s, name_r, lead_s, lead_r, share_s, share_r, small_s, small_r,
             wx_s, wx_r, wp_s, wp_r):
    r = lax.axis_index("rows")
    c = lax.axis_index("cols")
    half = rows // 2
    odd = r % 2
    pos = (1 - odd) * (r // 2) + odd * (rows - 1 - r // 2)

    def row_at(p):
        p = (p + rows) % rows
        upper = p // half
        return (1 - upper) * (2 * p) + upper * (2 * (rows - 1 - p) + 1)

    right = row_at(pos + 1)
    left = row_at(pos - 1)
    partner = c + 1 - 2 * (c % 2)

    def send(src, dst, s, v, row=None, col=None):
        return pltpu.make_async_remote_copy(
            src_ref=src, dst_ref=dst, send_sem=s, recv_sem=v,
            device_id=(r if row is None else row, c if col is None else col), device_id_type=MESH)

    barrier = pltpu.get_barrier_semaphore()
    for d in range(1, rows):
        pl.semaphore_signal(barrier, inc=1, device_id=((r + d) % rows, c), device_id_type=MESH)
    for d in range(1, cols):
        pl.semaphore_signal(barrier, inc=1, device_id=(r, (c + d) % cols), device_id_type=MESH)
    pl.semaphore_wait(barrier, rows + cols - 2)

    own_blocks = w_ref.shape[0]
    blocks = w_out.shape[0]
    height = own_ref.shape[1]
    slots = tile_ref.shape[0]
    cut = slots // 2
    part = (pl.ds(0, cut), pl.ds(cut, slots - cut))

    own = [pltpu.make_async_copy(tile_ref, tiles_out.at[r], local_sem.at[0]),
           pltpu.make_async_copy(names_ref, names_out.at[r], local_sem.at[1]),
           pltpu.make_async_copy(w_ref, w_out.at[pl.ds(c * own_blocks, own_blocks)], local_sem.at[2])]
    for copy in own:
        copy.start()

    waits = []
    for k in range(1, cols // 2):
        copy = send(w_ref, w_out.at[pl.ds(c * own_blocks, own_blocks)], wx_s.at[k], wx_r.at[k], col=(c + 2 * k) % cols)
        copy.start()
        waits.append(copy)
    copy = send(w_ref, w_out.at[pl.ds(c * own_blocks, own_blocks)], wp_s.at[0], wp_r.at[0], col=partner)
    copy.start()
    waits.append(copy)

    for d in range(1, rows):
        copy = send(names_ref, names_out.at[r], name_s.at[d], name_r.at[d], row=(r + d) % rows)
        copy.start()
        waits.append(copy)

    lead_row = [send(lead_ref, leads_out.at[c], lead_s.at[0], lead_r.at[0], row=right),
                send(lead_ref, leads_out.at[c], lead_s.at[1], lead_r.at[0], row=left)]

    @pl.when(r == 0)
    def _():
        for copy in lead_row:
            copy.start()
        for d in range(1, rows):
            send(small_ref, small_out, small_s.at[d], small_r.at[0], row=d).start()
        pltpu.make_async_copy(lead_ref, leads_out.at[c], local_sem.at[3]).start()
        pltpu.make_async_copy(small_ref, small_out, local_sem.at[4]).start()

    def first(h):
        send(tile_ref.at[part[h]], tiles_out.at[r, part[h]], fwd_s.at[0, h], fwd_r.at[0, h], row=right).start()
        send(tile_ref.at[part[h]], tiles_out.at[r, part[h]], bwd_s.at[0, h], bwd_r.at[0, h], row=left).start()

    first(0)
    near = jnp.minimum(pos, rows - pos)

    @pl.when(near >= 2)
    def _():
        first(1)

    def put_labels(dst, at, names):
        turned = jnp.transpose(names)
        for k in range(slots):
            dst[k, pl.ds(at, TILE), :] = jnp.broadcast_to(turned[:, k:k + 1], (TILE, TILE))

    for t in range(height // TILE):
        put_labels(label_own, t * TILE, own_names_ref[t])

    relay_right = send(leads_out.at[c], leads_out.at[c], lead_s.at[0], lead_r.at[0], row=right)
    relay_left = send(leads_out.at[c], leads_out.at[c], lead_s.at[1], lead_r.at[0], row=left)

    @pl.when(r != 0)
    def _():
        relay_right.wait_recv()

    @pl.when((pos >= 1) & (pos < half))
    def _():
        relay_right.start()

    @pl.when(pos >= half + 2)
    def _():
        relay_left.start()

    @pl.when(r == 0)
    def _():
        pltpu.make_async_copy(lead_ref, leads_out.at[c], local_sem.at[3]).wait()
        pltpu.make_async_copy(small_ref, small_out, local_sem.at[4]).wait()

    for d in range(1, cols):
        copy = send(leads_out.at[c], leads_out.at[c], share_s.at[d], share_r.at[d], col=(c + d) % cols)
        copy.start()
        waits.append(copy)

    @pl.when(near < 2)
    def _():
        first(1)

    last = half - 1

    def ring(s, h):
        ahead = row_at(pos - s)
        behind = row_at(pos + s)
        send(tile_ref.at[part[h]], tiles_out.at[r, part[h]], fwd_s.at[s - 1, h], fwd_r.at[s - 1, h], row=right).wait_recv()
        if s < last or h == 0:
            send(tiles_out.at[ahead, part[h]], tiles_out.at[ahead, part[h]], fwd_s.at[s, h], fwd_r.at[s, h], row=right).start()
        send(tile_ref.at[part[h]], tiles_out.at[r, part[h]], bwd_s.at[s - 1, h], bwd_r.at[s - 1, h], row=left).wait_recv()
        if s < last or h == 1:
            send(tiles_out.at[behind, part[h]], tiles_out.at[behind, part[h]], bwd_s.at[s, h], bwd_r.at[s, h], row=left).start()

    pending = [(s, h) for s in range(1, half) for h in range(2)]

    def serve(count):
        for _ in range(count):
            if pending:
                ring(*pending.pop(0))

    serve(2)
    for k in range(1, cols // 2):
        send(w_ref, w_out.at[pl.ds(c * own_blocks, own_blocks)], wx_s.at[k], wx_r.at[k], col=(c + 2 * k) % cols).wait_recv()
        source = (c + cols - 2 * k) % cols
        span = pl.ds(source * own_blocks, own_blocks)
        copy = send(w_out.at[span], w_out.at[span], wp_s.at[k], wp_r.at[k], col=partner)
        copy.start()
        waits.append(copy)
    for d in range(1, cols):
        send(leads_out.at[c], leads_out.at[c], share_s.at[d], share_r.at[d], col=(c + d) % cols).wait_recv()

    @pl.when(r != 0)
    def _():
        send(small_ref, small_out, small_s.at[0], small_r.at[0], row=0).wait_recv()

    for d in range(1, rows):
        send(names_ref, names_out.at[r], name_s.at[d], name_r.at[d], row=(r + d) % rows).wait_recv()
    for copy in own:
        copy.wait()
    chunk = TILE // cols
    for q in range(cols):
        lead_sc[:, q * chunk:(q + 1) * chunk, :] = leads_out[q]
    put_labels(label_own, height, small_out[0:8, :])
    for k in range(cols // 2):
        send(w_ref, w_out.at[pl.ds(c * own_blocks, own_blocks)], wp_s.at[k], wp_r.at[k], col=partner).wait_recv()
    serve(1)

    def weigh(b, carry):
        name = b.astype(jnp.float32)
        for t in range(height // TILE + 1):
            at = pl.ds(t * TILE, TILE)
            if t < height // TILE:
                coef = Rows(lambda k, lanes: own_ref[k, at, lanes], slots)
            else:
                coef = Rows(lambda k, lanes: lead_sc[k, :, lanes], slots)
            top, low = split(select_block(coef, lambda k: label_own[k, at, :], name))
            d_top[at, :] = top
            d_low[at, :] = low
        w_top, w_low = split(w_out[b])
        top, low = split(three(d_top[...], d_low[...], w_top, w_low, ((1,), (0,))))
        g_top[b] = top
        g_low[b] = low
        return carry

    middle = blocks // 2
    lax.fori_loop(0, middle, weigh, 0)
    serve(1)
    lax.fori_loop(middle, blocks, weigh, 0)
    serve(1)

    def group(tiles):
        width = len(tiles) * TILE
        for i, row in enumerate(tiles):
            put_labels(label_col, i * TILE, small_out[0:8, :] if row is None else names_out[row])
        acc[:, :width] = jnp.zeros((acc.shape[0], width), jnp.float32)

        def body(b, carry):
            name = b.astype(jnp.float32)
            for i, row in enumerate(tiles):
                at = pl.ds(i * TILE, TILE)
                if row is None:
                    coef = Rows(lambda k, lanes: lead_sc[k, :, lanes], slots)
                else:
                    coef = Rows(lambda k, lanes: tiles_out[row, k, :, lanes], slots)
                top, low = split(select_block(coef, lambda k: label_col[k, at, :], name))
                c_top[at, :] = top
                c_low[at, :] = low
            acc[:, :width] += three(g_top[b], g_low[b], c_top[:width, :], c_low[:width, :], ((1,), (1,)))
            return carry

        lax.fori_loop(0, blocks, body, 0)
        for i, row in enumerate(tiles):
            value = acc[:, i * TILE:(i + 1) * TILE]
            if row is None:
                lead_schur_out[...] = value
            else:
                schur_out[:, pl.ds(pl.multiple_of(row * TILE, TILE), TILE)] = value

    group([None, r])
    serve(1)

    lane = lax.broadcasted_iota(jnp.int32, (TILE, TILE), 1)
    line = lax.broadcasted_iota(jnp.int32, (TILE, TILE), 0)
    work[:, :TILE] = lead_schur_out[height:, :] + jnp.where(lane == line, jnp.broadcast_to(small_out[7:8, :], (TILE, TILE)), 0.0)
    work[:, TILE:] = jnp.where(lane == line, 1.0, 0.0)

    def eliminate(j, carry):
        pivot = work[pl.ds(j, 1), :]
        column = jnp.sum(jnp.where(lane == j, work[:, :TILE], 0.0), axis=1, keepdims=True)
        scale = jnp.sum(jnp.where(lane[0:1] == j, pivot[:, :TILE], 0.0), axis=1, keepdims=True)
        factor = jnp.where(line[:, 0:1] > j, column, 0.0) / scale
        work[...] = work[...] - factor * pivot
        return carry

    lax.fori_loop(0, TILE // 2, eliminate, 0)
    serve(1)
    lax.fori_loop(TILE // 2, TILE, eliminate, 0)
    diagonal = jnp.sum(jnp.where(lane == line, work[:, :TILE], 0.0), axis=1, keepdims=True)
    inverse_out[...] = work[:, TILE:] / jnp.sqrt(diagonal)

    for g in range(1, half):
        while pending and pending[0][0] <= g:
            serve(1)
        group([row_at(pos - g), row_at(pos + g)])
        serve(2)
    send(tile_ref.at[part[0]], tiles_out.at[r, part[0]], fwd_s.at[last, 0], fwd_r.at[last, 0], row=right).wait_recv()
    send(tile_ref.at[part[1]], tiles_out.at[r, part[1]], bwd_s.at[last, 1], bwd_r.at[last, 1], row=left).wait_recv()
    group([row_at(pos + half)])

    for s in range(half):
        for h in range(2):
            if s < last or h == 0:
                send(tile_ref.at[part[h]], tiles_out.at[r, part[h]], fwd_s.at[s, h], fwd_r.at[s, h], row=right).wait_send()
            if s < last or h == 1:
                send(tile_ref.at[part[h]], tiles_out.at[r, part[h]], bwd_s.at[s, h], bwd_r.at[s, h], row=left).wait_send()

    for copy in waits:
        copy.wait_send()
    @pl.when(r == 0)
    def _():
        for copy in lead_row:
            copy.wait_send()
        for d in range(1, rows):
            send(small_ref, small_out, small_s.at[d], small_r.at[0], row=d).wait_send()

    @pl.when((pos >= 1) & (pos < half))
    def _():
        relay_right.wait_send()

    @pl.when(pos >= half + 2)
    def _():
        relay_left.wait_send()


def assemble(rows, cols, tile, names, lead, small, weights, own, own_names):
    half = rows // 2
    dma = pltpu.SemaphoreType.DMA
    vmem = pl.BlockSpec(memory_space=pltpu.VMEM)
    slots, height, order = own.shape
    blocks = cols * weights.shape[0]
    tall = height + TILE
    f32, bf16 = jnp.float32, jnp.bfloat16
    return pl.pallas_call(
        functools.partial(exchange, rows, cols),
        out_shape=[
            jax.ShapeDtypeStruct((tall, rows * TILE), f32),
            jax.ShapeDtypeStruct((tall, TILE), f32),
            jax.ShapeDtypeStruct((TILE, TILE), f32),
            jax.ShapeDtypeStruct(small.shape, f32),
        ],
        in_specs=[vmem] * 7,
        out_specs=[vmem] * 4,
        scratch_shapes=[
            pltpu.VMEM((rows,) + tile.shape, f32),
            pltpu.VMEM((rows,) + names.shape, f32),
            pltpu.VMEM((cols,) + lead.shape, f32),
            pltpu.VMEM((blocks, order, order), f32),
            pltpu.VMEM((slots, tall, TILE), f32),
            pltpu.VMEM((slots, 2 * TILE, TILE), f32),
            pltpu.VMEM((slots, TILE, order), f32),
            pltpu.VMEM((tall, order), bf16),
            pltpu.VMEM((tall, order), bf16),
            pltpu.VMEM((2 * TILE, order), bf16),
            pltpu.VMEM((2 * TILE, order), bf16),
            pltpu.VMEM((blocks, tall, order), bf16),
            pltpu.VMEM((blocks, tall, order), bf16),
            pltpu.VMEM((tall, 2 * TILE), f32),
            pltpu.VMEM((TILE, 2 * TILE), f32),
        ]
        + [dma((5,))] + [dma((half, 2))] * 4 + [dma((rows,))] * 2 + [dma((2,)), dma((1,))]
        + [dma((cols,))] * 2 + [dma((rows,)), dma((1,))] + [dma((cols,))] * 4,
        compiler_params=pltpu.CompilerParams(collective_id=0, has_side_effects=True),
    )(tile, names, lead, small, weights, own, own_names)


def local(coefficients, support, primal, dual_inverse, block_sizes, damping, right_sides):
    col_index = lax.axis_index("cols")
    row_index = lax.axis_index("rows")
    rows = lax.axis_size("rows")
    cols = lax.axis_size("cols")
    layers, _, slots, order = coefficients.shape
    span = TILE * rows
    count_all = layers * span
    col_width = count_all // cols
    sides = right_sides.shape[1]
    positions = jnp.arange(order, dtype=jnp.int32)
    active = (positions[None, :] < block_sizes[:, None]).astype(jnp.float32)
    weights = primal * dual_inverse * active[:, :, None] * active[:, None, :]

    layer = (col_index * col_width) // span
    tile = jnp.transpose(lax.dynamic_index_in_dim(coefficients, layer, 0, keepdims=False), (1, 0, 2))
    own_names = jnp.pad(jnp.transpose(support, (0, 2, 1)).astype(jnp.float32), ((0, 0), (0, 8 - slots), (0, 0)))
    names = lax.dynamic_index_in_dim(own_names, layer, 0, keepdims=False)
    chunk = TILE // cols
    lead = jnp.transpose(lax.dynamic_slice_in_dim(coefficients[0], col_index * chunk, chunk, 0), (1, 0, 2))
    small = jnp.concatenate([
        own_names[0][:7],
        damping[0][None, :],
        jnp.pad(right_sides[0], ((0, -sides % 8), (0, 0)))], axis=0)
    own = jnp.transpose(coefficients, (2, 0, 1, 3)).reshape(slots, layers * TILE, order)
    schur_rows, own_lead, inverse, small = assemble(rows, cols, tile, names, lead, small, weights, own, own_names)
    if span != col_width:
        schur_rows = lax.dynamic_slice_in_dim(schur_rows, (col_index * col_width) % span, col_width, 1)
    lead_damping = small[7]
    top_sides = small[8:8 + sides]

    row_global = ((jnp.arange(layers)[:, None] * rows + row_index) * TILE + jnp.arange(TILE)[None, :]).reshape(-1)
    col_global = col_index * col_width + jnp.arange(col_width)
    flat_damping = damping.reshape(-1)
    schur = schur_rows[:layers * TILE] + jnp.where(row_global[:, None] == col_global[None, :], flat_damping[:, None], 0.0)
    lead_ids = jnp.arange(TILE)
    panel_raw = own_lead[:layers * TILE] + jnp.where(row_global[:, None] == lead_ids[None, :], flat_damping[:, None], 0.0)
    column_raw = schur_rows[layers * TILE:] + jnp.where(lead_ids[:, None] == col_global[None, :], lead_damping[:, None], 0.0)
    panel_factor = jnp.einsum("ak,jk->aj", panel_raw, inverse, precision=highest)
    column_panel = jnp.einsum("jk,kn->jn", inverse, column_raw, precision=highest)
    outer_term = jnp.dot(panel_factor, column_panel, precision=highest)
    row_later = row_global >= TILE
    col_later = col_global >= TILE
    updated = schur - jnp.where(row_later[:, None] & col_later[None, :], outer_term, 0.0)
    leading = jnp.einsum("sk,jk->sj", top_sides, inverse, precision=highest)
    panel_factor = panel_factor.reshape(layers, TILE, TILE)
    remainder = right_sides - jnp.einsum("sk,tak->tsa", leading, panel_factor, precision=highest)
    solved = jnp.where(row_later.reshape(layers, TILE)[:, None, :], remainder, leading[None, :, :])
    return (updated.reshape(layers, TILE, col_width), panel_factor, solved)


def solution(mesh):
    in_specs = (
        P(None, "rows", None, None),
        P(None, "rows", None),
        P("cols", None, None),
        P("cols", None, None),
        P("cols"),
        P(None, "rows"),
        P(None, "cols", "rows"),
    )
    out_specs = (P(None, "rows", "cols"), P(None, "rows", None), P(None, "cols", "rows"))
    return jax.shard_map(local, mesh=mesh, in_specs=in_specs, out_specs=out_specs, check_vma=False)
```

```python
import functools

import jax
import jax.numpy as jnp
from jax import lax
from jax.experimental import pallas as pl
from jax.experimental.pallas import tpu as pltpu
from jax.sharding import PartitionSpec as P

TILE = 128

MESH = pl.DeviceIdType.MESH
highest = lax.Precision.HIGHEST


def split(x):
    top = x.astype(jnp.bfloat16)
    return top, (x - top.astype(jnp.float32)).astype(jnp.bfloat16)


def product(a, b, dims):
    return lax.dot_general(a, b, (dims, ((), ())), preferred_element_type=jnp.float32)


def three(a_top, a_low, b_top, b_low, dims):
    return product(a_top, b_top, dims) + (product(a_top, b_low, dims) + product(a_low, b_top, dims))


def select_block(coef, label, b):
    pieces = []
    for h in range(0, 2):
        acc = None
        for k in range(coef.slots):
            hit = label(k) == b
            value = coef(k, h)
            acc = jnp.where(hit, value, jnp.zeros_like(value) if acc is None else acc)
        pieces.append(acc)
    return jnp.concatenate(pieces, axis=1)


class Rows:
    def __init__(self, read, slots):
        self.read, self.slots = read, slots

    def __call__(self, k, h):
        return self.read(k, pl.ds(h * TILE, TILE))


def exchange(rows, cols, small_ref, w_ref, own_ref, own_names_ref,
             schur_out, lead_schur_out, inverse_out, small_out,
             tiles_out, names_out, leads_out, w_out, label_own, label_col, lead_sc, d_top, d_low, c_top, c_low,
             g_top, g_low, acc, work,
             local_sem, fwd_s, fwd_r, bwd_s, bwd_r, name_s, name_r, lead_s, lead_r, share_s, share_r, small_s, small_r,
             wx_s, wx_r, wp_s, wp_r):
    r = lax.axis_index("rows")
    c = lax.axis_index("cols")
    half = rows // 2
    odd = r % 2
    pos = (1 - odd) * (r // 2) + odd * (rows - 1 - r // 2)

    def row_at(p):
        p = (p + rows) % rows
        upper = p // half
        return (1 - upper) * (2 * p) + upper * (2 * (rows - 1 - p) + 1)

    right = row_at(pos + 1)
    left = row_at(pos - 1)
    partner = c + 1 - 2 * (c % 2)

    def send(src, dst, s, v, row=None, col=None):
        return pltpu.make_async_remote_copy(
            src_ref=src, dst_ref=dst, send_sem=s, recv_sem=v,
            device_id=(r if row is None else row, c if col is None else col), device_id_type=MESH)

    barrier = pltpu.get_barrier_semaphore()
    for d in range(1, rows):
        pl.semaphore_signal(barrier, inc=1, device_id=((r + d) % rows, c), device_id_type=MESH)
    for d in range(1, cols):
        pl.semaphore_signal(barrier, inc=1, device_id=(r, (c + d) % cols), device_id_type=MESH)
    pl.semaphore_wait(barrier, rows + cols - 2)

    own_blocks = w_ref.shape[0]
    blocks = w_out.shape[0]
    height = own_ref.shape[1]
    slots = own_ref.shape[0]
    layer = (c * (height * rows // cols)) // (rows * TILE)
    tile_ref = own_ref.at[:, pl.ds(pl.multiple_of(layer * TILE, TILE), TILE)]
    names_ref = own_names_ref.at[layer]
    chunk = TILE // cols
    lead_ref = own_ref.at[:, pl.ds(pl.multiple_of(c * chunk, chunk), chunk)]
    cut = slots // 2
    part = (pl.ds(0, cut), pl.ds(cut, slots - cut))

    own = [pltpu.make_async_copy(tile_ref, tiles_out.at[r], local_sem.at[0]),
           pltpu.make_async_copy(names_ref, names_out.at[r], local_sem.at[1])]
    for copy in own:
        copy.start()

    waits = []
    def weight(source, i):
        return w_out.at[source * own_blocks + i]

    for i in range(own_blocks):
        copy = send(w_ref.at[i], weight(c, i), wp_s.at[0, i], wp_r.at[0, i], col=partner)
        copy.start()
        waits.append(copy)
        for k in range(1, cols // 2):
            copy = send(w_ref.at[i], weight(c, i), wx_s.at[k, i], wx_r.at[k, i], col=(c + 2 * k) % cols)
            copy.start()
            waits.append(copy)

    for d in range(1, rows):
        copy = send(names_ref, names_out.at[r], name_s.at[d], name_r.at[d], row=(r + d) % rows)
        copy.start()
        waits.append(copy)

    lead_row = [send(lead_ref, leads_out.at[c], lead_s.at[0], lead_r.at[0], row=right),
                send(lead_ref, leads_out.at[c], lead_s.at[1], lead_r.at[0], row=left)]

    @pl.when(r == 0)
    def _():
        for copy in lead_row:
            copy.start()
        for d in range(1, rows):
            send(small_ref, small_out, small_s.at[d], small_r.at[0], row=d).start()
        pltpu.make_async_copy(lead_ref, leads_out.at[c], local_sem.at[3]).start()
        pltpu.make_async_copy(small_ref, small_out, local_sem.at[4]).start()

    def first(h):
        send(tile_ref.at[part[h]], tiles_out.at[r, part[h]], fwd_s.at[0, h], fwd_r.at[0, h], row=right).start()
        send(tile_ref.at[part[h]], tiles_out.at[r, part[h]], bwd_s.at[0, h], bwd_r.at[0, h], row=left).start()

    first(0)
    near = jnp.minimum(pos, rows - pos)

    @pl.when(near >= 2)
    def _():
        first(1)

    def put_labels(dst, at, names):
        turned = jnp.transpose(names)
        for k in range(slots):
            dst[k, pl.ds(at, TILE), :] = jnp.broadcast_to(turned[:, k:k + 1], (TILE, TILE))

    for t in range(height // TILE):
        put_labels(label_own, t * TILE, own_names_ref[t])
    full = height // TILE

    def arrived(k, i):
        send(w_ref.at[i], weight(c, i), wp_s.at[k, i], wp_r.at[k, i], col=partner).wait_recv()

    def forward(i):
        if i < own_blocks:
            for k in range(1, cols // 2):
                send(w_ref.at[i], weight(c, i), wx_s.at[k, i], wx_r.at[k, i], col=(c + 2 * k) % cols).wait_recv()
                source = (c + cols - 2 * k) % cols
                copy = send(weight(source, i), weight(source, i), wp_s.at[k, i], wp_r.at[k, i], col=partner)
                copy.start()
                waits.append(copy)

    def weigh(source, held, tiles_high):
        first_tile, stop = tiles_high
        span = pl.ds(first_tile * TILE, (stop - first_tile) * TILE)
        for i in range(own_blocks):
            b = source * own_blocks + i
            name = b.astype(jnp.float32)
            side = i % 2
            for t in range(first_tile, stop):
                at = pl.ds(t * TILE, TILE)
                if t < full:
                    coef = Rows(lambda k, lanes: own_ref[k, at, lanes], slots)
                else:
                    coef = Rows(lambda k, lanes: lead_sc[k, :, lanes], slots)
                top, low = split(select_block(coef, lambda k: label_own[k, at, :], name))
                d_top[side, at, :] = top
                d_low[side, at, :] = low
            w_top, w_low = split(w_out[b] if held is None else held[i])
            top, low = split(three(d_top[side, span, :], d_low[side, span, :], w_top, w_low, ((1,), (0,))))
            g_top[b, span, :] = top
            g_low[b, span, :] = low

    weigh(c, w_ref, tiles_high=(0, full))

    relay_right = send(leads_out.at[c], leads_out.at[c], lead_s.at[0], lead_r.at[0], row=right)
    relay_left = send(leads_out.at[c], leads_out.at[c], lead_s.at[1], lead_r.at[0], row=left)

    @pl.when(r != 0)
    def _():
        relay_right.wait_recv()

    @pl.when((pos >= 1) & (pos < half))
    def _():
        relay_right.start()

    @pl.when(pos >= half + 2)
    def _():
        relay_left.start()

    @pl.when(r == 0)
    def _():
        pltpu.make_async_copy(lead_ref, leads_out.at[c], local_sem.at[3]).wait()
        pltpu.make_async_copy(small_ref, small_out, local_sem.at[4]).wait()

    for d in range(1, cols):
        copy = send(leads_out.at[c], leads_out.at[c], share_s.at[d], share_r.at[d], col=(c + d) % cols)
        copy.start()
        waits.append(copy)

    @pl.when(near < 2)
    def _():
        first(1)

    last = half - 1

    def ring(s, h):
        ahead = row_at(pos - s)
        behind = row_at(pos + s)
        send(tile_ref.at[part[h]], tiles_out.at[r, part[h]], fwd_s.at[s - 1, h], fwd_r.at[s - 1, h], row=right).wait_recv()
        if s < last or h == 0:
            send(tiles_out.at[ahead, part[h]], tiles_out.at[ahead, part[h]], fwd_s.at[s, h], fwd_r.at[s, h], row=right).start()
        send(tile_ref.at[part[h]], tiles_out.at[r, part[h]], bwd_s.at[s - 1, h], bwd_r.at[s - 1, h], row=left).wait_recv()
        if s < last or h == 1:
            send(tiles_out.at[behind, part[h]], tiles_out.at[behind, part[h]], bwd_s.at[s, h], bwd_r.at[s, h], row=left).start()

    for i in range(own_blocks):
        arrived(0, i)
    weigh(partner, None, tiles_high=(0, full))
    pending = [(s, h) for s in range(1, half) for h in range(2)]

    def serve(count):
        for _ in range(count):
            if pending:
                ring(*pending.pop(0))

    serve(2)
    forward(0)
    for d in range(1, cols):
        send(leads_out.at[c], leads_out.at[c], share_s.at[d], share_r.at[d], col=(c + d) % cols).wait_recv()

    @pl.when(r != 0)
    def _():
        send(small_ref, small_out, small_s.at[0], small_r.at[0], row=0).wait_recv()

    for d in range(1, rows):
        send(names_ref, names_out.at[r], name_s.at[d], name_r.at[d], row=(r + d) % rows).wait_recv()
    for copy in own:
        copy.wait()
    for q in range(cols):
        lead_sc[:, q * chunk:(q + 1) * chunk, :] = leads_out[q]
    put_labels(label_own, height, small_out[0:8, :])
    forward(1)
    weigh(c, w_ref, tiles_high=(full, full + 1))
    weigh(partner, None, tiles_high=(full, full + 1))
    serve(1)
    for i in range(2, own_blocks):
        forward(i)
    for k in range(1, cols // 2):
        weigh((c + cols - 2 * k) % cols, None, tiles_high=(0, full + 1))
        serve(1)
    for k in range(1, cols // 2):
        for i in range(own_blocks):
            arrived(k, i)
        weigh((partner + cols - 2 * k) % cols, None, tiles_high=(0, full + 1))
    serve(1)

    lane = lax.broadcasted_iota(jnp.int32, (TILE, TILE), 1)
    line = lax.broadcasted_iota(jnp.int32, (TILE, TILE), 0)

    def eliminate(j):
        at = jnp.minimum(j, TILE - 1)
        pivot = work[pl.ds(at, 1), :]
        column = jnp.sum(jnp.where(lane == at, work[:, :TILE], 0.0), axis=1, keepdims=True)
        scale = jnp.sum(jnp.where(lane[0:1] == at, pivot[:, :TILE], 0.0), axis=1, keepdims=True)
        factor = jnp.where(line[:, 0:1] > j, column, 0.0) / scale
        work[...] = work[...] - factor * pivot

    fold = max(u for u in range(1, 5) if blocks % u == 0)
    rounds = blocks // fold
    steps = -(-TILE // ((half - 1) * rounds))

    def group(tiles, step=None):
        width = len(tiles) * TILE
        for i, row in enumerate(tiles):
            put_labels(label_col, i * TILE, small_out[0:8, :] if row is None else names_out[row])
        acc[:, :width] = jnp.zeros((acc.shape[0], width), jnp.float32)

        def body(n, carry):
            for u in range(fold):
                name = (n * fold + u).astype(jnp.float32)
                for i, row in enumerate(tiles):
                    at = pl.ds(i * TILE, TILE)
                    if row is None:
                        coef = Rows(lambda k, lanes: lead_sc[k, :, lanes], slots)
                    else:
                        coef = Rows(lambda k, lanes: tiles_out[row, k, :, lanes], slots)
                    top, low = split(select_block(coef, lambda k: label_col[k, at, :], name))
                    c_top[u, at, :] = top
                    c_low[u, at, :] = low
            a_top = [g_top[n * fold + u] for u in range(fold)]
            a_low = [g_low[n * fold + u] for u in range(fold)]
            b_top = [c_top[u, :width, :] for u in range(fold)]
            b_low = [c_low[u, :width, :] for u in range(fold)]
            acc[:, :width] += product(
                jnp.concatenate(a_top + a_top + a_low, axis=1), jnp.concatenate(b_top + b_low + b_top, axis=1), ((1,), (1,)))
            if step is not None:
                for e in range(steps):
                    eliminate(step + n * steps + e)
            return carry

        lax.fori_loop(0, rounds, body, 0)
        for i, row in enumerate(tiles):
            value = acc[:, i * TILE:(i + 1) * TILE]
            if row is None:
                lead_schur_out[...] = value
            else:
                schur_out[:, pl.ds(pl.multiple_of(row * TILE, TILE), TILE)] = value

    group([None, r])
    serve(1)

    work[:, :TILE] = lead_schur_out[height:, :] + jnp.where(lane == line, jnp.broadcast_to(small_out[7:8, :], (TILE, TILE)), 0.0)
    work[:, TILE:] = jnp.where(lane == line, 1.0, 0.0)

    for g in range(1, half):
        while pending and pending[0][0] <= g:
            serve(1)
        group([row_at(pos - g), row_at(pos + g)], (g - 1) * rounds * steps)
        serve(2)
    send(tile_ref.at[part[0]], tiles_out.at[r, part[0]], fwd_s.at[last, 0], fwd_r.at[last, 0], row=right).wait_recv()
    send(tile_ref.at[part[1]], tiles_out.at[r, part[1]], bwd_s.at[last, 1], bwd_r.at[last, 1], row=left).wait_recv()
    diagonal = jnp.sum(jnp.where(lane == line, work[:, :TILE], 0.0), axis=1, keepdims=True)
    inverse_out[...] = work[:, TILE:] / jnp.sqrt(diagonal)
    group([row_at(pos + half)])

    for s in range(half):
        for h in range(2):
            if s < last or h == 0:
                send(tile_ref.at[part[h]], tiles_out.at[r, part[h]], fwd_s.at[s, h], fwd_r.at[s, h], row=right).wait_send()
            if s < last or h == 1:
                send(tile_ref.at[part[h]], tiles_out.at[r, part[h]], bwd_s.at[s, h], bwd_r.at[s, h], row=left).wait_send()

    for copy in waits:
        copy.wait_send()
    @pl.when(r == 0)
    def _():
        for copy in lead_row:
            copy.wait_send()
        for d in range(1, rows):
            send(small_ref, small_out, small_s.at[d], small_r.at[0], row=d).wait_send()

    @pl.when((pos >= 1) & (pos < half))
    def _():
        relay_right.wait_send()

    @pl.when(pos >= half + 2)
    def _():
        relay_left.wait_send()


def assemble(rows, cols, small, weights, own, own_names):
    half = rows // 2
    dma = pltpu.SemaphoreType.DMA
    vmem = pl.BlockSpec(memory_space=pltpu.VMEM)
    slots, height, order = own.shape
    blocks = cols * weights.shape[0]
    tall = height + TILE
    f32, bf16 = jnp.float32, jnp.bfloat16
    return pl.pallas_call(
        functools.partial(exchange, rows, cols),
        out_shape=[
            jax.ShapeDtypeStruct((tall, rows * TILE), f32),
            jax.ShapeDtypeStruct((tall, TILE), f32),
            jax.ShapeDtypeStruct((TILE, TILE), f32),
            jax.ShapeDtypeStruct(small.shape, f32),
        ],
        in_specs=[vmem] * 4,
        out_specs=[vmem] * 4,
        scratch_shapes=[
            pltpu.VMEM((rows, slots, TILE, order), f32),
            pltpu.VMEM((rows,) + own_names.shape[1:], f32),
            pltpu.VMEM((cols, slots, TILE // cols, order), f32),
            pltpu.VMEM((blocks, order, order), f32),
            pltpu.VMEM((slots, tall, TILE), f32),
            pltpu.VMEM((slots, 2 * TILE, TILE), f32),
            pltpu.VMEM((slots, TILE, order), f32),
            pltpu.VMEM((2, tall, order), bf16),
            pltpu.VMEM((2, tall, order), bf16),
            pltpu.VMEM((4, 2 * TILE, order), bf16),
            pltpu.VMEM((4, 2 * TILE, order), bf16),
            pltpu.VMEM((blocks, tall, order), bf16),
            pltpu.VMEM((blocks, tall, order), bf16),
            pltpu.VMEM((tall, 2 * TILE), f32),
            pltpu.VMEM((TILE, 2 * TILE), f32),
        ]
        + [dma((5,))] + [dma((half, 2))] * 4 + [dma((rows,))] * 2 + [dma((2,)), dma((1,))]
        + [dma((cols,))] * 2 + [dma((rows,)), dma((1,))] + [dma((cols, weights.shape[0]))] * 4,
        compiler_params=pltpu.CompilerParams(collective_id=0, has_side_effects=True),
    )(small, weights, own, own_names)


def local(coefficients, support, primal, dual_inverse, block_sizes, damping, right_sides):
    col_index = lax.axis_index("cols")
    row_index = lax.axis_index("rows")
    rows = lax.axis_size("rows")
    cols = lax.axis_size("cols")
    layers, _, slots, order = coefficients.shape
    span = TILE * rows
    count_all = layers * span
    col_width = count_all // cols
    sides = right_sides.shape[1]
    positions = jnp.arange(order, dtype=jnp.int32)
    active = (positions[None, :] < block_sizes[:, None]).astype(jnp.float32)
    weights = primal * dual_inverse * active[:, :, None] * active[:, None, :]

    own_names = jnp.pad(jnp.transpose(support, (0, 2, 1)).astype(jnp.float32), ((0, 0), (0, 8 - slots), (0, 0)))
    small = jnp.concatenate([
        own_names[0][:7],
        damping[0][None, :],
        jnp.pad(right_sides[0], ((0, -sides % 8), (0, 0)))], axis=0)
    own = jnp.transpose(coefficients, (2, 0, 1, 3)).reshape(slots, layers * TILE, order)
    schur_rows, own_lead, inverse, small = assemble(rows, cols, small, weights, own, own_names)
    if span != col_width:
        schur_rows = lax.dynamic_slice_in_dim(schur_rows, (col_index * col_width) % span, col_width, 1)
    lead_damping = small[7]
    top_sides = small[8:8 + sides]

    row_global = ((jnp.arange(layers)[:, None] * rows + row_index) * TILE + jnp.arange(TILE)[None, :]).reshape(-1)
    col_global = col_index * col_width + jnp.arange(col_width)
    flat_damping = damping.reshape(-1)
    schur = schur_rows[:layers * TILE] + jnp.where(row_global[:, None] == col_global[None, :], flat_damping[:, None], 0.0)
    lead_ids = jnp.arange(TILE)
    panel_raw = own_lead[:layers * TILE] + jnp.where(row_global[:, None] == lead_ids[None, :], flat_damping[:, None], 0.0)
    column_raw = schur_rows[layers * TILE:] + jnp.where(lead_ids[:, None] == col_global[None, :], lead_damping[:, None], 0.0)
    panel_factor = jnp.einsum("ak,jk->aj", panel_raw, inverse, precision=highest)
    column_panel = jnp.einsum("jk,kn->jn", inverse, column_raw, precision=highest)
    outer_term = jnp.dot(panel_factor, column_panel, precision=highest)
    row_later = row_global >= TILE
    col_later = col_global >= TILE
    updated = schur - jnp.where(row_later[:, None] & col_later[None, :], outer_term, 0.0)
    leading = jnp.einsum("sk,jk->sj", top_sides, inverse, precision=highest)
    panel_factor = panel_factor.reshape(layers, TILE, TILE)
    remainder = right_sides - jnp.einsum("sk,tak->tsa", leading, panel_factor, precision=highest)
    solved = jnp.where(row_later.reshape(layers, TILE)[:, None, :], remainder, leading[None, :, :])
    return (updated.reshape(layers, TILE, col_width), panel_factor, solved)


def solution(mesh):
    in_specs = (
        P(None, "rows", None, None),
        P(None, "rows", None),
        P("cols", None, None),
        P("cols", None, None),
        P("cols"),
        P(None, "rows"),
        P(None, "cols", "rows"),
    )
    out_specs = (P(None, "rows", "cols"), P(None, "rows", None), P(None, "cols", "rows"))
    return jax.shard_map(local, mesh=mesh, in_specs=in_specs, out_specs=out_specs, check_vma=False)
```

```python
import functools

import jax
import jax.numpy as jnp
from jax import lax
from jax.experimental import pallas as pl
from jax.experimental.pallas import tpu as pltpu
from jax.sharding import PartitionSpec as P

TILE = 128

MESH = pl.DeviceIdType.MESH
highest = lax.Precision.HIGHEST


def split(x):
    top = x.astype(jnp.bfloat16)
    return top, (x - top.astype(jnp.float32)).astype(jnp.bfloat16)


def product(a, b, dims):
    return lax.dot_general(a, b, (dims, ((), ())), preferred_element_type=jnp.float32)


def three(a_top, a_low, b_top, b_low, dims):
    return product(a_top, b_top, dims) + (product(a_top, b_low, dims) + product(a_low, b_top, dims))


def select_block(coef, label, b):
    pieces = []
    for h in range(0, 2):
        acc = None
        for k in range(coef.slots):
            hit = label(k) == b
            value = coef(k, h)
            acc = jnp.where(hit, value, jnp.zeros_like(value) if acc is None else acc)
        pieces.append(acc)
    return jnp.concatenate(pieces, axis=1)


class Rows:
    def __init__(self, read, slots):
        self.read, self.slots = read, slots

    def __call__(self, k, h):
        return self.read(k, pl.ds(h * TILE, TILE))


def exchange(rows, cols, small_ref, w_ref, own_ref, own_names_ref,
             schur_out, lead_schur_out, inverse_out, small_out,
             tiles_out, names_out, leads_out, w_out, label_own, label_col, lead_sc, d_top, d_low, c_top, c_low,
             g_top, g_low, acc, work,
             local_sem, fwd_s, fwd_r, bwd_s, bwd_r, name_s, name_r, lead_s, lead_r, share_s, share_r, small_s, small_r,
             wx_s, wx_r, wp_s, wp_r):
    r = lax.axis_index("rows")
    c = lax.axis_index("cols")
    half = rows // 2
    odd = r % 2
    pos = (1 - odd) * (r // 2) + odd * (rows - 1 - r // 2)

    def row_at(p):
        p = (p + rows) % rows
        upper = p // half
        return (1 - upper) * (2 * p) + upper * (2 * (rows - 1 - p) + 1)

    right = row_at(pos + 1)
    left = row_at(pos - 1)
    partner = c + 1 - 2 * (c % 2)

    def send(src, dst, s, v, row=None, col=None):
        return pltpu.make_async_remote_copy(
            src_ref=src, dst_ref=dst, send_sem=s, recv_sem=v,
            device_id=(r if row is None else row, c if col is None else col), device_id_type=MESH)

    barrier = pltpu.get_barrier_semaphore()
    for d in range(1, rows):
        pl.semaphore_signal(barrier, inc=1, device_id=((r + d) % rows, c), device_id_type=MESH)
    for d in range(1, cols):
        pl.semaphore_signal(barrier, inc=1, device_id=(r, (c + d) % cols), device_id_type=MESH)
    pl.semaphore_wait(barrier, rows + cols - 2)

    own_blocks = w_ref.shape[0]
    blocks = w_out.shape[0]
    height = own_ref.shape[1]
    slots = own_ref.shape[0]
    layer = (c * (height * rows // cols)) // (rows * TILE)
    tile_ref = own_ref.at[:, pl.ds(pl.multiple_of(layer * TILE, TILE), TILE)]
    names_ref = own_names_ref.at[layer]
    chunk = TILE // cols
    lead_ref = own_ref.at[:, pl.ds(pl.multiple_of(c * chunk, chunk), chunk)]
    cut = slots // 2
    part = (pl.ds(0, cut), pl.ds(cut, slots - cut))

    own = [pltpu.make_async_copy(tile_ref, tiles_out.at[r], local_sem.at[0]),
           pltpu.make_async_copy(names_ref, names_out.at[r], local_sem.at[1])]
    for copy in own:
        copy.start()

    waits = []
    def weight(source, i):
        return w_out.at[source * own_blocks + i]

    for i in range(own_blocks):
        copy = send(w_ref.at[i], weight(c, i), wp_s.at[0, i], wp_r.at[0, i], col=partner)
        copy.start()
        waits.append(copy)
        for k in range(1, cols // 2):
            copy = send(w_ref.at[i], weight(c, i), wx_s.at[k, i], wx_r.at[k, i], col=(c + 2 * k) % cols)
            copy.start()
            waits.append(copy)

    for d in range(1, rows):
        copy = send(names_ref, names_out.at[r], name_s.at[d], name_r.at[d], row=(r + d) % rows)
        copy.start()
        waits.append(copy)

    lead_row = [send(lead_ref, leads_out.at[c], lead_s.at[0], lead_r.at[0], row=right),
                send(lead_ref, leads_out.at[c], lead_s.at[1], lead_r.at[0], row=left)]

    @pl.when(r == 0)
    def _():
        for copy in lead_row:
            copy.start()
        for d in range(1, rows):
            send(small_ref, small_out, small_s.at[d], small_r.at[0], row=d).start()
        pltpu.make_async_copy(lead_ref, leads_out.at[c], local_sem.at[3]).start()
        pltpu.make_async_copy(small_ref, small_out, local_sem.at[4]).start()

    def first(h):
        send(tile_ref.at[part[h]], tiles_out.at[r, part[h]], fwd_s.at[0, h], fwd_r.at[0, h], row=right).start()
        send(tile_ref.at[part[h]], tiles_out.at[r, part[h]], bwd_s.at[0, h], bwd_r.at[0, h], row=left).start()

    first(0)
    near = jnp.minimum(pos, rows - pos)

    @pl.when(near >= 2)
    def _():
        first(1)

    def put_labels(dst, at, names):
        turned = jnp.transpose(names)
        for k in range(slots):
            dst[k, pl.ds(at, TILE), :] = jnp.broadcast_to(turned[:, k:k + 1], (TILE, TILE))

    for t in range(height // TILE):
        put_labels(label_own, t * TILE, own_names_ref[t])
    full = height // TILE

    def arrived(k, i):
        send(w_ref.at[i], weight(c, i), wp_s.at[k, i], wp_r.at[k, i], col=partner).wait_recv()

    def forward(i):
        if i < own_blocks:
            for k in range(1, cols // 2):
                send(w_ref.at[i], weight(c, i), wx_s.at[k, i], wx_r.at[k, i], col=(c + 2 * k) % cols).wait_recv()
                source = (c + cols - 2 * k) % cols
                copy = send(weight(source, i), weight(source, i), wp_s.at[k, i], wp_r.at[k, i], col=partner)
                copy.start()
                waits.append(copy)

    def weigh(source, held, tiles_high):
        first_tile, stop = tiles_high
        span = pl.ds(first_tile * TILE, (stop - first_tile) * TILE)
        for i in range(own_blocks):
            b = source * own_blocks + i
            name = b.astype(jnp.float32)
            side = i % 2
            for t in range(first_tile, stop):
                at = pl.ds(t * TILE, TILE)
                if t < full:
                    coef = Rows(lambda k, lanes: own_ref[k, at, lanes], slots)
                else:
                    coef = Rows(lambda k, lanes: lead_sc[k, :, lanes], slots)
                top, low = split(select_block(coef, lambda k: label_own[k, at, :], name))
                d_top[side, at, :] = top
                d_low[side, at, :] = low
            w_top, w_low = split(w_out[b] if held is None else held[i])
            top, low = split(three(d_top[side, span, :], d_low[side, span, :], w_top, w_low, ((1,), (0,))))
            g_top[b, span, :] = top
            g_low[b, span, :] = low

    weigh(c, w_ref, tiles_high=(0, full))

    relay_right = send(leads_out.at[c], leads_out.at[c], lead_s.at[0], lead_r.at[0], row=right)
    relay_left = send(leads_out.at[c], leads_out.at[c], lead_s.at[1], lead_r.at[0], row=left)

    @pl.when(r != 0)
    def _():
        relay_right.wait_recv()

    @pl.when((pos >= 1) & (pos < half))
    def _():
        relay_right.start()

    @pl.when(pos >= half + 2)
    def _():
        relay_left.start()

    @pl.when(r == 0)
    def _():
        pltpu.make_async_copy(lead_ref, leads_out.at[c], local_sem.at[3]).wait()
        pltpu.make_async_copy(small_ref, small_out, local_sem.at[4]).wait()

    for d in range(1, cols):
        copy = send(leads_out.at[c], leads_out.at[c], share_s.at[d], share_r.at[d], col=(c + d) % cols)
        copy.start()
        waits.append(copy)

    @pl.when(near < 2)
    def _():
        first(1)

    last = half - 1

    def ring(s, h):
        ahead = row_at(pos - s)
        behind = row_at(pos + s)
        send(tile_ref.at[part[h]], tiles_out.at[r, part[h]], fwd_s.at[s - 1, h], fwd_r.at[s - 1, h], row=right).wait_recv()
        if s < last or h == 0:
            send(tiles_out.at[ahead, part[h]], tiles_out.at[ahead, part[h]], fwd_s.at[s, h], fwd_r.at[s, h], row=right).start()
        send(tile_ref.at[part[h]], tiles_out.at[r, part[h]], bwd_s.at[s - 1, h], bwd_r.at[s - 1, h], row=left).wait_recv()
        if s < last or h == 1:
            send(tiles_out.at[behind, part[h]], tiles_out.at[behind, part[h]], bwd_s.at[s, h], bwd_r.at[s, h], row=left).start()

    for i in range(own_blocks):
        arrived(0, i)
    weigh(partner, None, tiles_high=(0, full))
    pending = [(s, h) for s in range(1, half) for h in range(2)]

    def serve(count):
        for _ in range(count):
            if pending:
                ring(*pending.pop(0))

    serve(2)
    forward(0)
    for d in range(1, cols):
        send(leads_out.at[c], leads_out.at[c], share_s.at[d], share_r.at[d], col=(c + d) % cols).wait_recv()

    @pl.when(r != 0)
    def _():
        send(small_ref, small_out, small_s.at[0], small_r.at[0], row=0).wait_recv()

    for d in range(1, rows):
        send(names_ref, names_out.at[r], name_s.at[d], name_r.at[d], row=(r + d) % rows).wait_recv()
    for copy in own:
        copy.wait()
    for q in range(cols):
        lead_sc[:, q * chunk:(q + 1) * chunk, :] = leads_out[q]
    put_labels(label_own, height, small_out[0:8, :])
    forward(1)
    weigh(c, w_ref, tiles_high=(full, full + 1))
    weigh(partner, None, tiles_high=(full, full + 1))
    serve(1)
    for i in range(2, own_blocks):
        forward(i)
    for k in range(1, cols // 2):
        weigh((c + cols - 2 * k) % cols, None, tiles_high=(0, full + 1))
        serve(1)
    for k in range(1, cols // 2):
        for i in range(own_blocks):
            arrived(k, i)
        weigh((partner + cols - 2 * k) % cols, None, tiles_high=(0, full + 1))

    lane = lax.broadcasted_iota(jnp.int32, (TILE, TILE), 1)
    line = lax.broadcasted_iota(jnp.int32, (TILE, TILE), 0)

    def eliminate(j):
        at = jnp.minimum(j, TILE - 1)
        pivot = work[pl.ds(at, 1), :]
        column = jnp.sum(jnp.where(lane == at, work[:, :TILE], 0.0), axis=1, keepdims=True)
        scale = jnp.sum(jnp.where(lane[0:1] == at, pivot[:, :TILE], 0.0), axis=1, keepdims=True)
        factor = jnp.where(line[:, 0:1] > j, column, 0.0) / scale
        work[...] = work[...] - factor * pivot

    fold = max(u for u in range(1, 5) if blocks % u == 0)
    rounds = blocks // fold
    steps = -(-TILE // ((half - 1) * rounds))

    def group(tiles, step=None):
        width = len(tiles) * TILE
        for i, row in enumerate(tiles):
            put_labels(label_col, i * TILE, small_out[0:8, :] if row is None else names_out[row])
        acc[:, :width] = jnp.zeros((acc.shape[0], width), jnp.float32)

        def body(n, carry):
            for u in range(fold):
                name = (n * fold + u).astype(jnp.float32)
                for i, row in enumerate(tiles):
                    at = pl.ds(i * TILE, TILE)
                    if row is None:
                        coef = Rows(lambda k, lanes: lead_sc[k, :, lanes], slots)
                    else:
                        coef = Rows(lambda k, lanes: tiles_out[row, k, :, lanes], slots)
                    top, low = split(select_block(coef, lambda k: label_col[k, at, :], name))
                    c_top[u, at, :] = top
                    c_low[u, at, :] = low
            a_top = [g_top[n * fold + u] for u in range(fold)]
            a_low = [g_low[n * fold + u] for u in range(fold)]
            b_top = [c_top[u, :width, :] for u in range(fold)]
            b_low = [c_low[u, :width, :] for u in range(fold)]
            acc[:, :width] += product(
                jnp.concatenate(a_top + a_top + a_low, axis=1), jnp.concatenate(b_top + b_low + b_top, axis=1), ((1,), (1,)))
            if step is not None:
                for e in range(steps):
                    eliminate(step + n * steps + e)
            return carry

        lax.fori_loop(0, rounds, body, 0)
        for i, row in enumerate(tiles):
            value = acc[:, i * TILE:(i + 1) * TILE]
            if row is None:
                lead_schur_out[...] = value
            else:
                schur_out[:, pl.ds(pl.multiple_of(row * TILE, TILE), TILE)] = value

    group([None, r])
    serve(1)

    work[:, :TILE] = lead_schur_out[height:, :] + jnp.where(lane == line, jnp.broadcast_to(small_out[7:8, :], (TILE, TILE)), 0.0)
    work[:, TILE:] = jnp.where(lane == line, 1.0, 0.0)

    for g in range(1, half):
        while pending and pending[0][0] <= g:
            serve(1)
        group([row_at(pos - g), row_at(pos + g)], (g - 1) * rounds * steps)
        serve(1)
    send(tile_ref.at[part[0]], tiles_out.at[r, part[0]], fwd_s.at[last, 0], fwd_r.at[last, 0], row=right).wait_recv()
    send(tile_ref.at[part[1]], tiles_out.at[r, part[1]], bwd_s.at[last, 1], bwd_r.at[last, 1], row=left).wait_recv()
    diagonal = jnp.sum(jnp.where(lane == line, work[:, :TILE], 0.0), axis=1, keepdims=True)
    inverse_out[...] = work[:, TILE:] / jnp.sqrt(diagonal)
    group([row_at(pos + half)])

    for s in range(half):
        for h in range(2):
            if s < last or h == 0:
                send(tile_ref.at[part[h]], tiles_out.at[r, part[h]], fwd_s.at[s, h], fwd_r.at[s, h], row=right).wait_send()
            if s < last or h == 1:
                send(tile_ref.at[part[h]], tiles_out.at[r, part[h]], bwd_s.at[s, h], bwd_r.at[s, h], row=left).wait_send()

    for copy in waits:
        copy.wait_send()
    @pl.when(r == 0)
    def _():
        for copy in lead_row:
            copy.wait_send()
        for d in range(1, rows):
            send(small_ref, small_out, small_s.at[d], small_r.at[0], row=d).wait_send()

    @pl.when((pos >= 1) & (pos < half))
    def _():
        relay_right.wait_send()

    @pl.when(pos >= half + 2)
    def _():
        relay_left.wait_send()


def assemble(rows, cols, small, weights, own, own_names):
    half = rows // 2
    dma = pltpu.SemaphoreType.DMA
    vmem = pl.BlockSpec(memory_space=pltpu.VMEM)
    slots, height, order = own.shape
    blocks = cols * weights.shape[0]
    tall = height + TILE
    f32, bf16 = jnp.float32, jnp.bfloat16
    return pl.pallas_call(
        functools.partial(exchange, rows, cols),
        out_shape=[
            jax.ShapeDtypeStruct((tall, rows * TILE), f32),
            jax.ShapeDtypeStruct((tall, TILE), f32),
            jax.ShapeDtypeStruct((TILE, TILE), f32),
            jax.ShapeDtypeStruct(small.shape, f32),
        ],
        in_specs=[vmem] * 4,
        out_specs=[vmem] * 4,
        scratch_shapes=[
            pltpu.VMEM((rows, slots, TILE, order), f32),
            pltpu.VMEM((rows,) + own_names.shape[1:], f32),
            pltpu.VMEM((cols, slots, TILE // cols, order), f32),
            pltpu.VMEM((blocks, order, order), f32),
            pltpu.VMEM((slots, tall, TILE), f32),
            pltpu.VMEM((slots, 2 * TILE, TILE), f32),
            pltpu.VMEM((slots, TILE, order), f32),
            pltpu.VMEM((2, tall, order), bf16),
            pltpu.VMEM((2, tall, order), bf16),
            pltpu.VMEM((4, 2 * TILE, order), bf16),
            pltpu.VMEM((4, 2 * TILE, order), bf16),
            pltpu.VMEM((blocks, tall, order), bf16),
            pltpu.VMEM((blocks, tall, order), bf16),
            pltpu.VMEM((tall, 2 * TILE), f32),
            pltpu.VMEM((TILE, 2 * TILE), f32),
        ]
        + [dma((5,))] + [dma((half, 2))] * 4 + [dma((rows,))] * 2 + [dma((2,)), dma((1,))]
        + [dma((cols,))] * 2 + [dma((rows,)), dma((1,))] + [dma((cols, weights.shape[0]))] * 4,
        compiler_params=pltpu.CompilerParams(collective_id=0, has_side_effects=True),
    )(small, weights, own, own_names)


def local(coefficients, support, primal, dual_inverse, block_sizes, damping, right_sides):
    col_index = lax.axis_index("cols")
    row_index = lax.axis_index("rows")
    rows = lax.axis_size("rows")
    cols = lax.axis_size("cols")
    layers, _, slots, order = coefficients.shape
    span = TILE * rows
    count_all = layers * span
    col_width = count_all // cols
    sides = right_sides.shape[1]
    positions = jnp.arange(order, dtype=jnp.int32)
    active = (positions[None, :] < block_sizes[:, None]).astype(jnp.float32)
    weights = primal * dual_inverse * active[:, :, None] * active[:, None, :]

    own_names = jnp.pad(jnp.transpose(support, (0, 2, 1)).astype(jnp.float32), ((0, 0), (0, 8 - slots), (0, 0)))
    small = jnp.concatenate([
        own_names[0][:7],
        damping[0][None, :],
        jnp.pad(right_sides[0], ((0, -sides % 8), (0, 0)))], axis=0)
    own = jnp.transpose(coefficients, (2, 0, 1, 3)).reshape(slots, layers * TILE, order)
    schur_rows, own_lead, inverse, small = assemble(rows, cols, small, weights, own, own_names)
    if span != col_width:
        schur_rows = lax.dynamic_slice_in_dim(schur_rows, (col_index * col_width) % span, col_width, 1)
    lead_damping = small[7]
    top_sides = small[8:8 + sides]

    row_global = ((jnp.arange(layers)[:, None] * rows + row_index) * TILE + jnp.arange(TILE)[None, :]).reshape(-1)
    col_global = col_index * col_width + jnp.arange(col_width)
    flat_damping = damping.reshape(-1)
    schur = schur_rows[:layers * TILE] + jnp.where(row_global[:, None] == col_global[None, :], flat_damping[:, None], 0.0)
    lead_ids = jnp.arange(TILE)
    panel_raw = own_lead[:layers * TILE] + jnp.where(row_global[:, None] == lead_ids[None, :], flat_damping[:, None], 0.0)
    column_raw = schur_rows[layers * TILE:] + jnp.where(lead_ids[:, None] == col_global[None, :], lead_damping[:, None], 0.0)
    panel_factor = jnp.einsum("ak,jk->aj", panel_raw, inverse, precision=highest)
    column_panel = jnp.einsum("jk,kn->jn", inverse, column_raw, precision=highest)
    outer_term = jnp.dot(panel_factor, column_panel, precision=highest)
    row_later = row_global >= TILE
    col_later = col_global >= TILE
    updated = schur - jnp.where(row_later[:, None] & col_later[None, :], outer_term, 0.0)
    leading = jnp.einsum("sk,jk->sj", top_sides, inverse, precision=highest)
    panel_factor = panel_factor.reshape(layers, TILE, TILE)
    remainder = right_sides - jnp.einsum("sk,tak->tsa", leading, panel_factor, precision=highest)
    solved = jnp.where(row_later.reshape(layers, TILE)[:, None, :], remainder, leading[None, :, :])
    return (updated.reshape(layers, TILE, col_width), panel_factor, solved)


def solution(mesh):
    in_specs = (
        P(None, "rows", None, None),
        P(None, "rows", None),
        P("cols", None, None),
        P("cols", None, None),
        P("cols"),
        P(None, "rows"),
        P(None, "cols", "rows"),
    )
    out_specs = (P(None, "rows", "cols"), P(None, "rows", None), P(None, "cols", "rows"))
    return jax.shard_map(local, mesh=mesh, in_specs=in_specs, out_specs=out_specs, check_vma=False)
```
